32 devices in a mesh: inst: 2 (over y), cell: 16 (over z, x, core).
Axes of the slice: x: 2, y: 2, z: 4, core: 2. Of those that a mesh axis runs over, the one named last changes fastest.
Arguments:
- adjoint: bfloat16 [4, 5, 32, 16, 256], P('inst', None, 'cell'), may hold values from -6 to 6
- flux_jac: bfloat16 [4, 5, 3, 32, 16, 256], P('inst', None, None, 'cell'), may hold values from -1.25 to 1.25
- shift: float32 [32, 16, 256], P('cell', 'inst'), may hold values from 0.1 to 2
Outputs:
- mesh_adjoint: float32 [3, 32, 16, 256], P(None, 'cell', 'inst')
- residual: float32 [3, 32, 16, 256], P(None, 'cell', 'inst')
The draws below stay inside these ranges and needn't reach their ends.
All inputs are finite; a program needn't handle non-finite values.
Results may differ from the reference program's by a relative error of at most 0.0003.
Values may be sent and summed in bfloat16 or wider, within the bound.
A program may use at most 64 MiB of HBM per device.

```python
import math
import jax
import jax.numpy as jnp
from jax import lax

NV = 5
NC = 3
ITERS = 3
NZ = 256
INSTANCES = 4
NX = 32
NY = 16


def strengthened(entries, key, source, target, parts, factor):
    owner, partner = [(jnp.arange(entries.shape[axis_at]) // (entries.shape[axis_at] // parts)).reshape([-1 if axis == axis_at else 1 for axis in range(entries.ndim)]) for axis_at in (source, target)]
    chosen = jax.random.permutation(key, parts)[partner]
    strong = (owner == chosen) | (owner == (partner + parts // 2) % parts)
    return jnp.where(strong, factor * entries, entries)


def steps_of(key, extent, cuts, low, top_value):
    gain = 1.0
    for axis_at, blocks in cuts:
        steps = jax.random.uniform(jax.random.fold_in(jax.random.fold_in(key, 6), axis_at), (blocks,), jnp.float32, low / len(cuts), top_value / len(cuts))
        gain = gain * jnp.repeat(jnp.exp(steps), extent[axis_at] // blocks).reshape((-1,) + (1,) * (len(extent) - 1 - axis_at))
    return gain


def bell_draw(key, shape, spread, reach, split=(), kind=jnp.bfloat16):
    drawn = jax.random.normal(key, shape, jnp.float32) * spread
    if len(split) > 0:
        drawn = steps_of(key, shape, split, -0.22, 0.18) * drawn
    return jnp.clip(drawn, min=-reach, max=reach).astype(kind)


def heavy_noise(rng, extent, spread, reach, split, heavy, dtype=jnp.bfloat16):
    array = spread * jax.random.normal(rng, extent, jnp.float32)
    if split:
        array = array * steps_of(rng, extent, split, -0.22, 0.18)
    return jnp.clip(strengthened(array, jax.random.fold_in(rng, 3), *heavy), -reach, reach).astype(dtype)


def setup_inputs(seed: int = 0) -> dict:
    splits = jax.random.split(jax.random.key(seed), 4)
    return {
        "adjoint": bell_draw(splits[0], (INSTANCES, NV, NX, NY, NZ), 1.0, 6.0, ((0, 2), (2, 16))),
        "flux_jac": heavy_noise(splits[1], (INSTANCES, NV, NC, NX, NY, NZ), (2 * NV * INSTANCES) ** -0.5, 1.25, ((0, 2), (3, 16)), (0, 4, 2, 2.0)),
        "shift": jnp.clip(jnp.exp(math.log(2.0) - 2.9957323 * jax.random.uniform(splits[2], (NX, NY, NZ), jnp.float32) ** steps_of(splits[2], (NX, NY, NZ), ((0, 16), (1, 2)), -0.2, 0.2)), 0.1, 2.0),
    }


mu_shear = 1.0
lame_first = 1.5


def instance_term(total, pair):
    adjoint_one, flux_one = pair
    padded = jnp.pad(adjoint_one.astype(jnp.float32), ((0, 0), (1, 1), (0, 0), (0, 0)))
    flux_full = flux_one.astype(jnp.float32)
    upper = jnp.einsum("vkxyz,vxyz->kxyz", flux_full, padded[:, 2:], precision=lax.Precision.HIGHEST)
    lower = jnp.einsum("vkxyz,vxyz->kxyz", flux_full, padded[:, :-2], precision=lax.Precision.HIGHEST)
    return total + (upper - lower), None


def operate(field, shift):
    padded = jnp.pad(field, ((0, 0), (1, 1), (1, 1), (1, 1)))
    beside = padded[:, 2:, 1:-1, 1:-1] + padded[:, :-2, 1:-1, 1:-1]
    beside = beside + padded[:, 1:-1, 2:, 1:-1] + padded[:, 1:-1, :-2, 1:-1]
    beside = beside + padded[:, 1:-1, 1:-1, 2:] + padded[:, 1:-1, 1:-1, :-2]
    diverge = (padded[0, 2:, 1:-1, 1:-1] - field[0]) + (padded[1, 1:-1, 2:, 1:-1] - field[1]) + (padded[2, 1:-1, 1:-1, 2:] - field[2])
    low_pad = jnp.pad(diverge, ((1, 0), (1, 0), (1, 0)))
    grad_part = jnp.stack([low_pad[:-1, 1:, 1:] - diverge, low_pad[1:, :-1, 1:] - diverge, low_pad[1:, 1:, :-1] - diverge])
    return mu_shear * (6.0 * field - beside) + shift * field + lame_first * grad_part


def reference(adjoint, flux_jac, shift):
    start = jnp.zeros((NC, NX, NY, NZ), jnp.float32)
    sens, _ = lax.scan(instance_term, start, (adjoint, flux_jac))
    mesh_adjoint = jnp.zeros_like(sens)
    residual, direction = sens, sens
    norm_now = jnp.sum(residual * residual)
    for sweep in range(ITERS):
        image = operate(direction, shift)
        alpha = norm_now / jnp.sum(direction * image)
        mesh_adjoint = mesh_adjoint + alpha * direction
        residual = residual - alpha * image
        norm_next = jnp.sum(residual * residual)
        direction = residual + (norm_next / norm_now) * direction
        norm_now = norm_next
    return mesh_adjoint, residual
```

```python
import functools

import jax
import jax.numpy as jnp
from jax import lax
from jax.experimental import pallas as pl
from jax.experimental.pallas import tpu as pltpu
from jax.sharding import PartitionSpec as P

ITERS = 3
LAME = 1.5
CENTER = 10.0
SPREAD = 8.0
HALO = 3
MESH = pl.DeviceIdType.MESH
F32 = jnp.float32


def remote(src, dst, send_sem, recv_sem, device):
    return pltpu.make_async_remote_copy(
        src_ref=src,
        dst_ref=dst,
        send_sem=send_sem,
        recv_sem=recv_sem,
        device_id=device,
        device_id_type=MESH,
    )


def apply_operator(src, dst, sh, lo, hi, valid_row, edges):
    y_first, y_last, z_first, z_last = edges
    wy, nz = src.shape[2], src.shape[3]

    def up_y(v):
        return jnp.where(y_last, 0.0, pltpu.roll(v, wy - 1, 0))

    def down_y(v):
        return jnp.where(y_first, 0.0, pltpu.roll(v, 1, 0))

    def up_z(v):
        return jnp.where(z_last, 0.0, pltpu.roll(v, nz - 1, 1))

    def down_z(v):
        return jnp.where(z_first, 0.0, pltpu.roll(v, 1, 1))

    before = None
    for row in range(lo - 1, hi + 1):
        fields = [src[k, row] for k in range(3)]
        uy, uz = up_y(fields[1]), up_z(fields[2])
        dv = (src[0, row + 1] - fields[0]) + (uy - fields[1]) + (uz - fields[2])
        dv = jnp.where(valid_row(row), dv, 0.0)
        if row >= lo:
            diag = sh[row - 1] + (6.0 - CENTER)
            shifted = [before, down_y(dv), down_z(dv)]
            for k in range(3):
                u = fields[k]
                beside = src[k, row - 1] + src[k, row + 1]
                beside = beside + (uy if k == 1 else up_y(u)) + down_y(u)
                beside = beside + (uz if k == 2 else up_z(u)) + down_z(u)
                out = (diag * u - beside + LAME * (shifted[k] - dv)) * (1.0 / SPREAD)
                dst[k, row] = jnp.where(valid_row(row), out, 0.0)
        before = dv


def coefficients(mu):
    def inner(a, b, skip=0):
        total = None
        for p, x in enumerate(a):
            for q, y in enumerate(b):
                if x is None or y is None:
                    continue
                term = x * y * mu[p + q]
                total = term if total is None else total + term
        return total

    def times(a):
        return [
            (CENTER * a[j] if j < len(a) else 0.0) + (SPREAD * a[j - 1] if j > 0 else 0.0)
            for j in range(len(a) + 1)
        ]

    one = jnp.ones_like(mu[0])
    solution_at, residual, direction = [], [one], [one]
    norm_now = mu[0]
    for sweep in range(ITERS):
        image = times(direction)
        alpha = norm_now / inner(direction, image)
        solution_at = [
            (solution_at[j] if j < len(solution_at) else 0.0) + alpha * direction[j]
            for j in range(len(direction))
        ]
        residual = [
            (residual[j] if j < len(residual) else 0.0) - alpha * image[j]
            for j in range(len(image))
        ]
        if sweep + 1 < ITERS:
            norm_next = inner(residual, residual)
            ratio = norm_next / norm_now
            direction = [
                residual[j] + (ratio * direction[j] if j < len(direction) else 0.0)
                for j in range(len(residual))
            ]
            norm_now = norm_next
    return solution_at, residual


def kernel(
    n_inst, n_cell, cols, window,
    adj_hbm, flux_hbm, shift_hbm, x_ref, r_ref,
    adj, flux, halo, part, got, u0, u1, u2, u3, sh, row_out, gath, gath2,
    load_sem, halo_send, halo_recv, sh_send, sh_recv, y_send, y_recv,
    x_send, x_recv, g_send, g_recv, h_send, h_recv,
):
    i, c = lax.axis_index("inst"), lax.axis_index("cell")
    wy = window * cols
    nv = adj.shape[0] * adj.shape[1]
    nz = adj.shape[-1]

    def start_of(j):
        return jnp.clip(j - 1, 0, n_inst - window)

    own_at = pl.multiple_of((i - start_of(i)) * cols, cols)

    loads = [
        pltpu.make_async_copy(adj_hbm, adj, load_sem.at[0]),
        pltpu.make_async_copy(flux_hbm, flux, load_sem.at[1]),
        pltpu.make_async_copy(shift_hbm, sh.at[pl.ds(2, 2), pl.ds(own_at, cols)], load_sem.at[2]),
    ]
    for load in loads:
        load.start()

    barrier = pltpu.get_barrier_semaphore()
    for d in range(1, n_cell):
        pl.semaphore_signal(barrier, inc=1, device_id=(i, lax.rem(c + d, n_cell)), device_id_type=MESH)
    for d in range(1, n_inst):
        pl.semaphore_signal(barrier, inc=1, device_id=(lax.rem(i + d, n_inst), c), device_id_type=MESH)
    expected = n_cell - 1 + n_inst - 1
    for dj in range(-(window - 1), window):
        if dj == 0:
            continue
        for dc in (-1, 1):
            there = (i + dj >= 0) & (i + dj < n_inst) & (c + dc >= 0) & (c + dc < n_cell)
            expected = expected + jnp.where(there, 1, 0)

            @pl.when(there)
            def _():
                pl.semaphore_signal(barrier, inc=1, device_id=(i + dj, c + dc), device_id_type=MESH)

    pl.semaphore_wait(barrier, expected)

    def halo_copy(dc):
        side = 0 if dc == 1 else 1
        return remote(
            adj_hbm.at[:, :, 1 if dc == 1 else 0], halo.at[side],
            halo_send.at[side], halo_recv.at[side], (i, c + dc),
        )

    def inside(dc):
        return (c + dc >= 0) & (c + dc < n_cell)

    for dc in (1, -1):
        @pl.when(inside(dc))
        def _():
            halo_copy(dc).start()

    def sh_copy(dj, dc):
        j = i + dj
        slot = jnp.clip(i - start_of(j), 0, window - 1)
        at = pl.multiple_of(slot * cols, cols)
        return remote(
            shift_hbm, sh.at[pl.ds(2 - 2 * dc, 2), pl.ds(at, cols)],
            sh_send.at[dj + window - 1, dc + 1], sh_recv.at[slot, dc + 1], (j, c + dc),
        )

    def sh_valid(dj, dc):
        j = i + dj
        first = start_of(j)
        return (j >= 0) & (j < n_inst) & inside(dc) & (i >= first) & (i < first + window)

    sh_moves = [
        (dj, dc)
        for dj in range(-(window - 1), window)
        for dc in (-1, 0, 1)
        if (dj, dc) != (0, 0)
    ]
    for dj, dc in sh_moves:
        @pl.when(sh_valid(dj, dc))
        def _():
            sh_copy(dj, dc).start()

    @pl.when(c == 0)
    def _():
        halo[0] = jnp.zeros_like(halo[0])
        sh[0:2] = jnp.zeros_like(sh[0:2])
        u0[:, 0:3] = jnp.zeros_like(u0[:, 0:3])

    @pl.when(c == 1)
    def _():
        u0[:, 0:1] = jnp.zeros_like(u0[:, 0:1])

    @pl.when(c == n_cell - 1)
    def _():
        halo[1] = jnp.zeros_like(halo[1])
        sh[4:6] = jnp.zeros_like(sh[4:6])
        u0[:, 5:8] = jnp.zeros_like(u0[:, 5:8])

    @pl.when(c == n_cell - 2)
    def _():
        u0[:, 7:8] = jnp.zeros_like(u0[:, 7:8])

    loads[0].wait()
    loads[1].wait()

    n_v = adj.shape[1]

    def own_terms(k):
        for y0 in range(0, adj.shape[3], 16):
            ys = slice(y0, y0 + 16)
            low, high = None, None
            for v in range(nv):
                a, b = v // n_v, v % n_v
                t0 = flux[a, b, k, 0, ys].astype(F32) * adj[a, b, 1, ys].astype(F32)
                t1 = flux[a, b, k, 1, ys].astype(F32) * adj[a, b, 0, ys].astype(F32)
                low = t0 if low is None else low + t0
                high = t1 if high is None else high + t1
            part[k, 0, ys] = low
            part[k, 1, ys] = -high

    def halo_terms(k):
        for y0 in range(0, adj.shape[3], 16):
            ys = slice(y0, y0 + 16)
            low, high = part[k, 0, ys], part[k, 1, ys]
            for v in range(nv):
                a, b = v // n_v, v % n_v
                low = low - flux[a, b, k, 0, ys].astype(F32) * halo[0, a, b, ys].astype(F32)
                high = high + flux[a, b, k, 1, ys].astype(F32) * halo[1, a, b, ys].astype(F32)
            part[k, 0, ys] = low
            part[k, 1, ys] = high

    for k in range(3):
        own_terms(k)

    for dc in (1, -1):
        @pl.when(inside(-dc))
        def _():
            halo_copy(dc).wait_recv()

    def y_copy(k, d):
        j = lax.rem(i + d, n_inst)
        at = pl.multiple_of(start_of(j) * cols, cols)
        return remote(
            part.at[k, :, pl.ds(at, wy)], got.at[d - 1, k],
            y_send.at[d - 1, k], y_recv.at[d - 1, k], (j, c),
        )

    for k in range(3):
        halo_terms(k)
        for d in range(1, n_inst):
            y_copy(k, d).start()

    x_moves = {1: (3, 1, 2), -1: (3, 5, 2), 2: (4, 0, 1), -2: (3, 7, 1)}

    def x_copy(k, dc):
        src, dst, rows = x_moves[dc]
        slot = sorted(x_moves).index(dc)
        return remote(
            u0.at[k, pl.ds(src, rows)], u0.at[k, pl.ds(dst, rows)],
            x_send.at[slot, k], x_recv.at[slot, k], (i, c + dc),
        )

    my_at = pl.multiple_of(start_of(i) * cols, cols)
    for k in range(3):
        for d in range(1, n_inst):
            y_copy(k, d).wait_recv()
        total = part[k, :, pl.ds(my_at, wy)]
        for d in range(1, n_inst):
            total = total + got[d - 1, k]
        u0[k, 3:5] = total
        for dc in x_moves:
            @pl.when(inside(dc))
            def _():
                x_copy(k, dc).start()

    loads[2].wait()
    for dj, dc in sh_moves:
        @pl.when(sh_valid(dj, dc))
        def _():
            sh_copy(dj, dc).wait_send()
    for slot in range(window):
        for dc in (-1, 0, 1):
            owner = start_of(i) + slot
            there = inside(-dc)
            if dc == 0:
                there = there & (owner != i)

            @pl.when(there)
            def _():
                at = slot * cols
                remote(
                    shift_hbm, sh.at[pl.ds(2 - 2 * dc, 2), pl.ds(at, cols)],
                    sh_send.at[0, 0], sh_recv.at[slot, dc + 1], (i, c),
                ).wait_recv()

    for k in range(3):
        for dc in x_moves:
            @pl.when(inside(-dc))
            def _():
                x_copy(k, dc).wait_recv()

    shape = (wy, nz)
    y_at = lax.broadcasted_iota(jnp.int32, shape, 0)
    z_at = lax.broadcasted_iota(jnp.int32, shape, 1)
    edges = (y_at == 0, y_at == wy - 1, z_at == 0, z_at == nz - 1)

    def valid_row(row):
        place = 2 * c + row - HALO
        return (place >= 0) & (place < 2 * n_cell)

    apply_operator(u0, u1, sh, 1, 6, valid_row, edges)
    apply_operator(u1, u2, sh, 2, 5, valid_row, edges)
    apply_operator(u2, u3, sh, 3, 4, valid_row, edges)

    basis = (u0, u1, u2, u3)
    lane = lax.broadcasted_iota(jnp.int32, (1, 128), 1)
    packed = jnp.zeros((1, 128), F32)
    for m in range(6):
        a, b = basis[m // 2], basis[(m + 1) // 2]
        total = None
        for k in range(3):
            for row in (3, 4):
                term = a[k, row] * b[k, row]
                total = term if total is None else total + term
        if window < n_inst:
            total = jnp.where((y_at >= own_at) & (y_at < own_at + cols), total, 0.0)
        value = jnp.sum(jnp.sum(total, axis=0, keepdims=True), axis=1, keepdims=True)
        packed = jnp.where(lane == m, value, packed)

    def gather_sum(packed, slot, buffer, send, recv, count, device):
        row_out[slot] = packed
        moves = [
            remote(row_out.at[slot], buffer.at[d - 1], send.at[d - 1], recv.at[d - 1], device(d))
            for d in range(1, count)
        ]
        for move in moves:
            move.start()
        total = packed
        for d, move in enumerate(moves):
            move.wait_recv()
            total = total + buffer[d]
        for move in moves:
            move.wait_send()
        return total

    packed = gather_sum(
        packed, 0, gath, g_send, g_recv, n_cell, lambda d: (i, lax.rem(c + d, n_cell))
    )
    if window < n_inst:
        packed = gather_sum(
            packed, 1, gath2, h_send, h_recv, n_inst, lambda d: (lax.rem(i + d, n_inst), c)
        )
    mu = [
        jnp.sum(jnp.where(lane == m, packed, 0.0), axis=1, keepdims=True) for m in range(6)
    ]
    at_x, at_r = coefficients(mu)

    own = pl.ds(own_at, cols)
    for k in range(3):
        for row in range(2):
            b = [basis[j][k, row + 3, own] for j in range(4)]
            x_ref[k, row] = at_x[0] * b[0] + at_x[1] * b[1] + at_x[2] * b[2]
            r_ref[k, row] = at_r[0] * b[0] + at_r[1] * b[1] + at_r[2] * b[2] + at_r[3] * b[3]

    for dc in (1, -1):
        @pl.when(inside(dc))
        def _():
            halo_copy(dc).wait_send()
    for k in range(3):
        for d in range(1, n_inst):
            y_copy(k, d).wait_send()
        for dc in x_moves:
            @pl.when(inside(dc))
            def _():
                x_copy(k, dc).wait_send()


def local(n_inst, n_cell, adjoint, flux_jac, shift):
    rows, cols, nz = shift.shape
    ny = adjoint.shape[3]
    window = min(3, n_inst)
    wy = window * cols
    field = pltpu.VMEM((3, rows + 2 * HALO, wy, nz), F32)
    dma = pltpu.SemaphoreType.DMA
    out = jax.ShapeDtypeStruct((3, rows, cols, nz), F32)
    peers = max(n_inst - 1, 1)
    return pl.pallas_call(
        functools.partial(kernel, n_inst, n_cell, cols, window),
        out_shape=(out, out),
        in_specs=[pl.BlockSpec(memory_space=pl.ANY)] * 3,
        out_specs=(pl.BlockSpec(memory_space=pltpu.VMEM),) * 2,
        scratch_shapes=[
            pltpu.VMEM(adjoint.shape, adjoint.dtype),
            pltpu.VMEM(flux_jac.shape, flux_jac.dtype),
            pltpu.VMEM((2,) + adjoint.shape[:2] + (ny, nz), adjoint.dtype),
            pltpu.VMEM((3, rows, ny, nz), F32),
            pltpu.VMEM((peers, 3, rows, wy, nz), F32),
            field, field, field, field,
            pltpu.VMEM((rows + 4, wy, nz), F32),
            pltpu.VMEM((2, 1, 128), F32),
            pltpu.VMEM((n_cell - 1, 1, 128), F32),
            pltpu.VMEM((peers, 1, 128), F32),
            dma((3,)),
            dma((2,)), dma((2,)),
            dma((2 * window - 1, 3)), dma((window, 3)),
            dma((peers, 3)), dma((peers, 3)),
            dma((4, 3)), dma((4, 3)),
            dma((n_cell - 1,)), dma((n_cell - 1,)),
            dma((peers,)), dma((peers,)),
        ],
        compiler_params=pltpu.CompilerParams(collective_id=0, has_side_effects=True),
    )(adjoint, flux_jac, shift)


def solution(mesh):
    placed = (
        P("inst", None, "cell", None, None),
        P("inst", None, None, "cell", None, None),
        P("cell", "inst", None),
    )
    return jax.shard_map(
        functools.partial(local, mesh.shape["inst"], mesh.shape["cell"]),
        mesh=mesh,
        in_specs=placed,
        out_specs=(P(None, "cell", "inst", None), P(None, "cell", "inst", None)),
        check_vma=False,
    )
```

```python
import functools

import jax
import jax.numpy as jnp
from jax import lax
from jax.experimental import pallas as pl
from jax.experimental.pallas import tpu as pltpu
from jax.sharding import PartitionSpec as P

ITERS = 3
LAME = 1.5
CENTER = 10.0
SPREAD = 8.0
HALO = 3
VMEM_GRANT = 24 << 20
MESH = pl.DeviceIdType.MESH
F32 = jnp.float32


def remote(src, dst, send_sem, recv_sem, device):
    return pltpu.make_async_remote_copy(
        src_ref=src,
        dst_ref=dst,
        send_sem=send_sem,
        recv_sem=recv_sem,
        device_id=device,
        device_id_type=MESH,
    )


def apply_operator(src, dst, sh, lo, hi, valid_row, edges):
    y_first, y_last, z_first, z_last = edges
    wy, nz = src.shape[2], src.shape[3]

    def up_y(v):
        return jnp.where(y_last, 0.0, pltpu.roll(v, wy - 1, 0))

    def down_y(v):
        return jnp.where(y_first, 0.0, pltpu.roll(v, 1, 0))

    def up_z(v):
        return jnp.where(z_last, 0.0, pltpu.roll(v, nz - 1, 1))

    def down_z(v):
        return jnp.where(z_first, 0.0, pltpu.roll(v, 1, 1))

    before = None
    for row in range(lo - 1, hi + 1):
        fields = [src[k, row] for k in range(3)]
        uy, uz = up_y(fields[1]), up_z(fields[2])
        dv = (src[0, row + 1] - fields[0]) + (uy - fields[1]) + (uz - fields[2])
        dv = jnp.where(valid_row(row), dv, 0.0)
        if row >= lo:
            diag = sh[row - 1] + (6.0 - CENTER)
            shifted = [before, down_y(dv), down_z(dv)]
            for k in range(3):
                u = fields[k]
                beside = src[k, row - 1] + src[k, row + 1]
                beside = beside + (uy if k == 1 else up_y(u)) + down_y(u)
                beside = beside + (uz if k == 2 else up_z(u)) + down_z(u)
                out = (diag * u - beside + LAME * (shifted[k] - dv)) * (1.0 / SPREAD)
                dst[k, row] = jnp.where(valid_row(row), out, 0.0)
        before = dv


def coefficients(mu):
    def inner(a, b, skip=0):
        total = None
        for p, x in enumerate(a):
            for q, y in enumerate(b):
                if x is None or y is None:
                    continue
                term = x * y * mu[p + q]
                total = term if total is None else total + term
        return total

    def times(a):
        return [
            (CENTER * a[j] if j < len(a) else 0.0) + (SPREAD * a[j - 1] if j > 0 else 0.0)
            for j in range(len(a) + 1)
        ]

    one = jnp.ones_like(mu[0])
    solution_at, residual, direction = [], [one], [one]
    norm_now = mu[0]
    for sweep in range(ITERS):
        image = times(direction)
        alpha = norm_now / inner(direction, image)
        solution_at = [
            (solution_at[j] if j < len(solution_at) else 0.0) + alpha * direction[j]
            for j in range(len(direction))
        ]
        residual = [
            (residual[j] if j < len(residual) else 0.0) - alpha * image[j]
            for j in range(len(image))
        ]
        if sweep + 1 < ITERS:
            norm_next = inner(residual, residual)
            ratio = norm_next / norm_now
            direction = [
                residual[j] + (ratio * direction[j] if j < len(direction) else 0.0)
                for j in range(len(residual))
            ]
            norm_now = norm_next
    return solution_at, residual


def kernel(
    n_inst, n_cell, cols, window,
    adj_hbm, flux_hbm, shift_hbm, x_ref, r_ref,
    adj, flux, halo, part, got, u0, u1, u2, u3, sh, row_out, gath, gath2,
    load_sem, halo_send, halo_recv, sh_send, sh_recv, y_send, y_recv,
    x_send, x_recv, g_send, g_recv, h_send, h_recv, near,
):
    i, c = lax.axis_index("inst"), lax.axis_index("cell")
    wy = window * cols
    nv = adj.shape[0] * adj.shape[1]
    nz = adj.shape[-1]

    def start_of(j):
        return jnp.clip(j - 1, 0, n_inst - window)

    own_at = pl.multiple_of((i - start_of(i)) * cols, cols)

    loads = [
        pltpu.make_async_copy(adj_hbm, adj, load_sem.at[0]),
        pltpu.make_async_copy(flux_hbm, flux, load_sem.at[1]),
        pltpu.make_async_copy(shift_hbm, sh.at[pl.ds(2, 2), pl.ds(own_at, cols)], load_sem.at[2]),
    ]
    for load in loads:
        load.start()

    def inside(dc):
        return (c + dc >= 0) & (c + dc < n_cell)

    barrier = pltpu.get_barrier_semaphore()
    expected = n_inst - 1
    for dc in (-1, 1, -2, 2):
        expected = expected + jnp.where(inside(dc), 1, 0)

        @pl.when(inside(dc))
        def _():
            pl.semaphore_signal(barrier, inc=1, device_id=(i, c + dc), device_id_type=MESH)

    for d in range(1, n_inst):
        pl.semaphore_signal(barrier, inc=1, device_id=(lax.rem(i + d, n_inst), c), device_id_type=MESH)
    pl.semaphore_wait(barrier, expected)

    reaches = [r for r in (2, 4, 8, 16, 32, 64) if r < n_cell]

    def hello(number):
        if number < len(reaches):
            for dc in (-reaches[number], reaches[number]):
                @pl.when(inside(dc))
                def _():
                    pl.semaphore_signal(
                        near.at[number], inc=1, device_id=(i, c + dc), device_id_type=MESH
                    )

    def heard(number):
        if number < len(reaches):
            count = 0
            for dc in (-reaches[number], reaches[number]):
                count = count + jnp.where(inside(dc), 1, 0)
            pl.semaphore_wait(near.at[number], count)

    def halo_copy(dc):
        side = 0 if dc == 1 else 1
        return remote(
            adj_hbm.at[:, :, 1 if dc == 1 else 0], halo.at[side],
            halo_send.at[side], halo_recv.at[side], (i, c + dc),
        )

    for dc in (1, -1):
        @pl.when(inside(dc))
        def _():
            halo_copy(dc).start()
    hello(0)

    def sh_copy(dj, dc):
        j = i + dj
        slot = jnp.clip(i - start_of(j), 0, window - 1)
        at = pl.multiple_of(slot * cols, cols)
        return remote(
            shift_hbm, sh.at[pl.ds(2 - 2 * dc, 2), pl.ds(at, cols)],
            sh_send.at[dj + window - 1, dc + 1], sh_recv.at[slot, dc + 1], (j, c + dc),
        )

    def sh_valid(dj, dc):
        j = i + dj
        first = start_of(j)
        return (j >= 0) & (j < n_inst) & inside(dc) & (i >= first) & (i < first + window)

    sh_moves = [
        (dj, dc)
        for dj in range(-(window - 1), window)
        for dc in (-1, 0, 1)
        if (dj, dc) != (0, 0)
    ]
    def sh_start(columns_only):
        for dj, dc in sh_moves:
            if (dc == 0) == columns_only:
                @pl.when(sh_valid(dj, dc))
                def _():
                    sh_copy(dj, dc).start()

    sh_start(True)

    @pl.when(c == 0)
    def _():
        halo[0] = jnp.zeros_like(halo[0])
        sh[0:2] = jnp.zeros_like(sh[0:2])
        u0[:, 0:3] = jnp.zeros_like(u0[:, 0:3])

    @pl.when(c == 1)
    def _():
        u0[:, 0:1] = jnp.zeros_like(u0[:, 0:1])

    @pl.when(c == n_cell - 1)
    def _():
        halo[1] = jnp.zeros_like(halo[1])
        sh[4:6] = jnp.zeros_like(sh[4:6])
        u0[:, 5:8] = jnp.zeros_like(u0[:, 5:8])

    @pl.when(c == n_cell - 2)
    def _():
        u0[:, 7:8] = jnp.zeros_like(u0[:, 7:8])

    loads[0].wait()
    loads[1].wait()

    n_v = adj.shape[1]

    def own_terms(k):
        for y0 in range(0, adj.shape[3], 16):
            ys = slice(y0, y0 + 16)
            low, high = None, None
            for v in range(nv):
                a, b = v // n_v, v % n_v
                t0 = flux[a, b, k, 0, ys].astype(F32) * adj[a, b, 1, ys].astype(F32)
                t1 = flux[a, b, k, 1, ys].astype(F32) * adj[a, b, 0, ys].astype(F32)
                low = t0 if low is None else low + t0
                high = t1 if high is None else high + t1
            part[k, 0, ys] = low
            part[k, 1, ys] = -high

    def halo_terms(k):
        for y0 in range(0, adj.shape[3], 16):
            ys = slice(y0, y0 + 16)
            low, high = part[k, 0, ys], part[k, 1, ys]
            for v in range(nv):
                a, b = v // n_v, v % n_v
                low = low - flux[a, b, k, 0, ys].astype(F32) * halo[0, a, b, ys].astype(F32)
                high = high + flux[a, b, k, 1, ys].astype(F32) * halo[1, a, b, ys].astype(F32)
            part[k, 0, ys] = low
            part[k, 1, ys] = high

    for k in range(3):
        own_terms(k)
    heard(0)
    hello(1)

    for dc in (1, -1):
        @pl.when(inside(-dc))
        def _():
            halo_copy(dc).wait_recv()

    sh_start(False)
    heard(1)
    hello(2)

    def y_copy(k, d):
        j = lax.rem(i + d, n_inst)
        at = pl.multiple_of(start_of(j) * cols, cols)
        return remote(
            part.at[k, :, pl.ds(at, wy)], got.at[d - 1, k],
            y_send.at[d - 1, k], y_recv.at[d - 1, k], (j, c),
        )

    for k in range(3):
        halo_terms(k)
        for d in range(1, n_inst):
            y_copy(k, d).start()

    x_moves = {1: (3, 1, 2), -1: (3, 5, 2), 2: (4, 0, 1), -2: (3, 7, 1)}

    def x_copy(k, dc):
        src, dst, rows = x_moves[dc]
        slot = sorted(x_moves).index(dc)
        return remote(
            u0.at[k, pl.ds(src, rows)], u0.at[k, pl.ds(dst, rows)],
            x_send.at[slot, k], x_recv.at[slot, k], (i, c + dc),
        )

    my_at = pl.multiple_of(start_of(i) * cols, cols)
    for k in range(3):
        for d in range(1, n_inst):
            y_copy(k, d).wait_recv()
        total = part[k, :, pl.ds(my_at, wy)]
        for d in range(1, n_inst):
            total = total + got[d - 1, k]
        u0[k, 3:5] = total
        for dc in x_moves:
            @pl.when(inside(dc))
            def _():
                x_copy(k, dc).start()

    for number in range(2, len(reaches)):
        heard(number)
        hello(number + 1)

    loads[2].wait()
    for dj, dc in sh_moves:
        @pl.when(sh_valid(dj, dc))
        def _():
            sh_copy(dj, dc).wait_send()
    for slot in range(window):
        for dc in (-1, 0, 1):
            owner = start_of(i) + slot
            there = inside(-dc)
            if dc == 0:
                there = there & (owner != i)

            @pl.when(there)
            def _():
                at = slot * cols
                remote(
                    shift_hbm, sh.at[pl.ds(2 - 2 * dc, 2), pl.ds(at, cols)],
                    sh_send.at[0, 0], sh_recv.at[slot, dc + 1], (i, c),
                ).wait_recv()

    for k in range(3):
        for dc in x_moves:
            @pl.when(inside(-dc))
            def _():
                x_copy(k, dc).wait_recv()

    shape = (wy, nz)
    y_at = lax.broadcasted_iota(jnp.int32, shape, 0)
    z_at = lax.broadcasted_iota(jnp.int32, shape, 1)
    edges = (y_at == 0, y_at == wy - 1, z_at == 0, z_at == nz - 1)

    def valid_row(row):
        place = 2 * c + row - HALO
        return (place >= 0) & (place < 2 * n_cell)

    apply_operator(u0, u1, sh, 1, 6, valid_row, edges)
    apply_operator(u1, u2, sh, 2, 5, valid_row, edges)
    apply_operator(u2, u3, sh, 3, 4, valid_row, edges)

    basis = (u0, u1, u2, u3)
    lane = lax.broadcasted_iota(jnp.int32, (1, 128), 1)
    packed = jnp.zeros((1, 128), F32)
    for m in range(6):
        a, b = basis[m // 2], basis[(m + 1) // 2]
        total = None
        for k in range(3):
            for row in (3, 4):
                term = a[k, row] * b[k, row]
                total = term if total is None else total + term
        if window < n_inst:
            total = jnp.where((y_at >= own_at) & (y_at < own_at + cols), total, 0.0)
        value = jnp.sum(jnp.sum(total, axis=0, keepdims=True), axis=1, keepdims=True)
        packed = jnp.where(lane == m, value, packed)

    def gather_sum(packed, slot, buffer, send, recv, count, device):
        row_out[slot] = packed
        moves = [
            remote(row_out.at[slot], buffer.at[d - 1], send.at[d - 1], recv.at[d - 1], device(d))
            for d in range(1, count)
        ]
        for move in moves:
            move.start()
        total = packed
        for d, move in enumerate(moves):
            move.wait_recv()
            total = total + buffer[d]
        for move in moves:
            move.wait_send()
        return total

    packed = gather_sum(
        packed, 0, gath, g_send, g_recv, n_cell, lambda d: (i, lax.rem(c + d, n_cell))
    )
    if window < n_inst:
        packed = gather_sum(
            packed, 1, gath2, h_send, h_recv, n_inst, lambda d: (lax.rem(i + d, n_inst), c)
        )
    mu = [
        jnp.sum(jnp.where(lane == m, packed, 0.0), axis=1, keepdims=True) for m in range(6)
    ]
    at_x, at_r = coefficients(mu)

    own = pl.ds(own_at, cols)
    for k in range(3):
        for row in range(2):
            b = [basis[j][k, row + 3, own] for j in range(4)]
            x_ref[k, row] = at_x[0] * b[0] + at_x[1] * b[1] + at_x[2] * b[2]
            r_ref[k, row] = at_r[0] * b[0] + at_r[1] * b[1] + at_r[2] * b[2] + at_r[3] * b[3]

    for dc in (1, -1):
        @pl.when(inside(dc))
        def _():
            halo_copy(dc).wait_send()
    for k in range(3):
        for d in range(1, n_inst):
            y_copy(k, d).wait_send()
        for dc in x_moves:
            @pl.when(inside(dc))
            def _():
                x_copy(k, dc).wait_send()


def hand_over(x_in, r_in, x_out, r_out, sem):
    moves = [
        pltpu.make_async_copy(x_in, x_out, sem.at[0]),
        pltpu.make_async_copy(r_in, r_out, sem.at[1]),
    ]
    for move in moves:
        move.start()
    for move in moves:
        move.wait()


def local(n_inst, n_cell, adjoint, flux_jac, shift):
    rows, cols, nz = shift.shape
    ny = adjoint.shape[3]
    window = min(3, n_inst)
    wy = window * cols
    field = pltpu.VMEM((3, rows + 2 * HALO, wy, nz), F32)
    dma = pltpu.SemaphoreType.DMA
    out = jax.ShapeDtypeStruct((3, rows, cols, nz), F32)
    peers = max(n_inst - 1, 1)
    answers = pl.pallas_call(
        functools.partial(kernel, n_inst, n_cell, cols, window),
        out_shape=(out, out),
        in_specs=[pl.BlockSpec(memory_space=pltpu.HBM)] * 3,
        out_specs=(pl.BlockSpec(memory_space=pltpu.VMEM),) * 2,
        scratch_shapes=[
            pltpu.VMEM(adjoint.shape, adjoint.dtype),
            pltpu.VMEM(flux_jac.shape, flux_jac.dtype),
            pltpu.VMEM((2,) + adjoint.shape[:2] + (ny, nz), adjoint.dtype),
            pltpu.VMEM((3, rows, ny, nz), F32),
            pltpu.VMEM((peers, 3, rows, wy, nz), F32),
            field, field, field, field,
            pltpu.VMEM((rows + 4, wy, nz), F32),
            pltpu.VMEM((2, 1, 128), F32),
            pltpu.VMEM((n_cell - 1, 1, 128), F32),
            pltpu.VMEM((peers, 1, 128), F32),
            dma((3,)),
            dma((2,)), dma((2,)),
            dma((2 * window - 1, 3)), dma((window, 3)),
            dma((peers, 3)), dma((peers, 3)),
            dma((4, 3)), dma((4, 3)),
            dma((n_cell - 1,)), dma((n_cell - 1,)),
            dma((peers,)), dma((peers,)),
            pltpu.SemaphoreType.REGULAR((6,)),
        ],
        compiler_params=pltpu.CompilerParams(
            collective_id=0, has_side_effects=True, vmem_limit_bytes=VMEM_GRANT
        ),
    )(*[pltpu.with_memory_space_constraint(a, pltpu.HBM) for a in (adjoint, flux_jac, shift)])
    return pl.pallas_call(
        hand_over,
        out_shape=(out, out),
        in_specs=[pl.BlockSpec(memory_space=pltpu.VMEM)] * 2,
        out_specs=(pl.BlockSpec(memory_space=pltpu.HBM),) * 2,
        scratch_shapes=[dma((2,))],
        compiler_params=pltpu.CompilerParams(vmem_limit_bytes=1 << 20),
    )(*answers)


def solution(mesh):
    placed = (
        P("inst", None, "cell", None, None),
        P("inst", None, None, "cell", None, None),
        P("cell", "inst", None),
    )
    return jax.shard_map(
        functools.partial(local, mesh.shape["inst"], mesh.shape["cell"]),
        mesh=mesh,
        in_specs=placed,
        out_specs=(P(None, "cell", "inst", None), P(None, "cell", "inst", None)),
        check_vma=False,
    )
```

```python
import functools

import jax
import jax.numpy as jnp
from jax import lax
from jax.experimental import pallas as pl
from jax.experimental.pallas import tpu as pltpu
from jax.sharding import PartitionSpec as P

ITERS = 3
LAME = 1.5
CENTER = 10.0
SPREAD = 8.0
HALO = 3
VMEM_GRANT = 24 << 20
MESH = pl.DeviceIdType.MESH
F32 = jnp.float32


def remote(src, dst, send_sem, recv_sem, device):
    return pltpu.make_async_remote_copy(
        src_ref=src,
        dst_ref=dst,
        send_sem=send_sem,
        recv_sem=recv_sem,
        device_id=device,
        device_id_type=MESH,
    )


def apply_operator(src, dst, sh, lo, hi, valid_row, edges):
    y_first, y_last, z_first, z_last = edges
    wy, nz = src.shape[2], src.shape[3]

    def up_y(v):
        return jnp.where(y_last, 0.0, pltpu.roll(v, wy - 1, 0))

    def down_y(v):
        return jnp.where(y_first, 0.0, pltpu.roll(v, 1, 0))

    def up_z(v):
        return jnp.where(z_last, 0.0, pltpu.roll(v, nz - 1, 1))

    def down_z(v):
        return jnp.where(z_first, 0.0, pltpu.roll(v, 1, 1))

    before = None
    for row in range(lo - 1, hi + 1):
        fields = [src[k, row] for k in range(3)]
        uy, uz = up_y(fields[1]), up_z(fields[2])
        dv = (src[0, row + 1] - fields[0]) + (uy - fields[1]) + (uz - fields[2])
        dv = jnp.where(valid_row(row), dv, 0.0)
        if row >= lo:
            diag = sh[row - 1] + (6.0 - CENTER)
            shifted = [before, down_y(dv), down_z(dv)]
            for k in range(3):
                u = fields[k]
                beside = src[k, row - 1] + src[k, row + 1]
                beside = beside + (uy if k == 1 else up_y(u)) + down_y(u)
                beside = beside + (uz if k == 2 else up_z(u)) + down_z(u)
                out = (diag * u - beside + LAME * (shifted[k] - dv)) * (1.0 / SPREAD)
                dst[k, row] = jnp.where(valid_row(row), out, 0.0)
        before = dv


def coefficients(mu):
    def inner(a, b, skip=0):
        total = None
        for p, x in enumerate(a):
            for q, y in enumerate(b):
                if x is None or y is None:
                    continue
                term = x * y * mu[p + q]
                total = term if total is None else total + term
        return total

    def times(a):
        return [
            (CENTER * a[j] if j < len(a) else 0.0) + (SPREAD * a[j - 1] if j > 0 else 0.0)
            for j in range(len(a) + 1)
        ]

    one = jnp.ones_like(mu[0])
    solution_at, residual, direction = [], [one], [one]
    norm_now = mu[0]
    for sweep in range(ITERS):
        image = times(direction)
        alpha = norm_now / inner(direction, image)
        solution_at = [
            (solution_at[j] if j < len(solution_at) else 0.0) + alpha * direction[j]
            for j in range(len(direction))
        ]
        residual = [
            (residual[j] if j < len(residual) else 0.0) - alpha * image[j]
            for j in range(len(image))
        ]
        if sweep + 1 < ITERS:
            norm_next = inner(residual, residual)
            ratio = norm_next / norm_now
            direction = [
                residual[j] + (ratio * direction[j] if j < len(direction) else 0.0)
                for j in range(len(residual))
            ]
            norm_now = norm_next
    return solution_at, residual


def kernel(
    n_inst, n_cell, cols, window,
    adj_hbm, flux_hbm, shift_hbm, x_ref, r_ref,
    adj, flux, halo, part, got, u0, u1, u2, u3, sh, row_out, gath, gath2,
    load_sem, halo_send, halo_recv, sh_send, sh_recv, y_send, y_recv,
    x_send, x_recv, g_send, g_recv, h_send, h_recv, near, shx_send, shx_recv,
):
    i, c = lax.axis_index("inst"), lax.axis_index("cell")
    wy = window * cols
    nv = adj.shape[0] * adj.shape[1]
    nz = adj.shape[-1]

    halves = 2 if nz % 256 == 0 else 1

    def lanes(h):
        return slice(h * (nz // halves), (h + 1) * (nz // halves))

    def start_of(j):
        return jnp.clip(j - 1, 0, n_inst - window)

    own_at = pl.multiple_of((i - start_of(i)) * cols, cols)

    loads = [
        pltpu.make_async_copy(adj_hbm, adj, load_sem.at[0]),
        pltpu.make_async_copy(flux_hbm, flux, load_sem.at[1]),
        pltpu.make_async_copy(shift_hbm, sh.at[pl.ds(2, 2), pl.ds(own_at, cols)], load_sem.at[2]),
    ]
    for load in loads:
        load.start()

    def inside(dc):
        return (c + dc >= 0) & (c + dc < n_cell)

    barrier = pltpu.get_barrier_semaphore()
    expected = n_inst - 1
    for dc in (-1, 1, -2, 2):
        expected = expected + jnp.where(inside(dc), 1, 0)

        @pl.when(inside(dc))
        def _():
            pl.semaphore_signal(barrier, inc=1, device_id=(i, c + dc), device_id_type=MESH)

    for d in range(1, n_inst):
        pl.semaphore_signal(barrier, inc=1, device_id=(lax.rem(i + d, n_inst), c), device_id_type=MESH)
    pl.semaphore_wait(barrier, expected)

    reaches = [r for r in (2, 4, 8, 16, 32, 64) if r < n_cell]

    def hello(number):
        if number < len(reaches):
            for dc in (-reaches[number], reaches[number]):
                @pl.when(inside(dc))
                def _():
                    pl.semaphore_signal(
                        near.at[number], inc=1, device_id=(i, c + dc), device_id_type=MESH
                    )

    def heard(number):
        if number < len(reaches):
            count = 0
            for dc in (-reaches[number], reaches[number]):
                count = count + jnp.where(inside(dc), 1, 0)
            pl.semaphore_wait(near.at[number], count)

    def halo_copy(dc, h):
        side = 0 if dc == 1 else 1
        return remote(
            adj.at[:, :, 1 if dc == 1 else 0, :, lanes(h)], halo.at[side, :, :, :, lanes(h)],
            halo_send.at[side, h], halo_recv.at[side, h], (i, c + dc),
        )

    loads[0].wait()

    for h in range(halves):
        for dc in (1, -1):
            @pl.when(inside(dc))
            def _():
                halo_copy(dc, h).start()
    hello(0)

    def sh_copy(dj, dc):
        j = i + dj
        slot = jnp.clip(i - start_of(j), 0, window - 1)
        at = pl.multiple_of(slot * cols, cols)
        return remote(
            shift_hbm, sh.at[pl.ds(2 - 2 * dc, 2), pl.ds(at, cols)],
            sh_send.at[dj + window - 1, dc + 1], sh_recv.at[slot, dc + 1], (j, c + dc),
        )

    def sh_valid(dj, dc):
        j = i + dj
        first = start_of(j)
        return (j >= 0) & (j < n_inst) & inside(dc) & (i >= first) & (i < first + window)

    sh_moves = [(dj, 0) for dj in range(-(window - 1), window) if dj != 0]
    for dj, dc in sh_moves:
        @pl.when(sh_valid(dj, dc))
        def _():
            sh_copy(dj, dc).start()

    def sh_rows_copy(dc):
        side = 0 if dc == 1 else 1
        return remote(
            sh.at[2:4], sh.at[pl.ds(2 - 2 * dc, 2)],
            shx_send.at[side], shx_recv.at[side], (i, c + dc),
        )

    def shift_rows():
        loads[2].wait()
        for slot in range(window):
            @pl.when(start_of(i) + slot != i)
            def _():
                remote(
                    shift_hbm, sh.at[2:4, pl.ds(slot * cols, cols)],
                    sh_send.at[0, 0], sh_recv.at[slot, 1], (i, c),
                ).wait_recv()
        for dc in (1, -1):
            @pl.when(inside(dc))
            def _():
                sh_rows_copy(dc).start()

    @pl.when(c == 0)
    def _():
        halo[0] = jnp.zeros_like(halo[0])
        sh[0:2] = jnp.zeros_like(sh[0:2])
        u0[:, 0:3] = jnp.zeros_like(u0[:, 0:3])

    @pl.when(c == 1)
    def _():
        u0[:, 0:1] = jnp.zeros_like(u0[:, 0:1])

    @pl.when(c == n_cell - 1)
    def _():
        halo[1] = jnp.zeros_like(halo[1])
        sh[4:6] = jnp.zeros_like(sh[4:6])
        u0[:, 5:8] = jnp.zeros_like(u0[:, 5:8])

    @pl.when(c == n_cell - 2)
    def _():
        u0[:, 7:8] = jnp.zeros_like(u0[:, 7:8])

    loads[1].wait()

    n_v = adj.shape[1]

    def own_terms(k):
        for y0 in range(0, adj.shape[3], 16):
            ys = slice(y0, y0 + 16)
            low, high = None, None
            for v in range(nv):
                a, b = v // n_v, v % n_v
                t0 = flux[a, b, k, 0, ys].astype(F32) * adj[a, b, 1, ys].astype(F32)
                t1 = flux[a, b, k, 1, ys].astype(F32) * adj[a, b, 0, ys].astype(F32)
                low = t0 if low is None else low + t0
                high = t1 if high is None else high + t1
            part[k, 0, ys] = low
            part[k, 1, ys] = -high

    def halo_terms(k, h):
        ls = lanes(h)
        for y0 in range(0, adj.shape[3], 16):
            ys = slice(y0, y0 + 16)
            low, high = part[k, 0, ys, ls], part[k, 1, ys, ls]
            for v in range(nv):
                a, b = v // n_v, v % n_v
                f0, f1 = flux[a, b, k, 0, ys, ls], flux[a, b, k, 1, ys, ls]
                low = low - f0.astype(F32) * halo[0, a, b, ys, ls].astype(F32)
                high = high + f1.astype(F32) * halo[1, a, b, ys, ls].astype(F32)
            part[k, 0, ys, ls] = low
            part[k, 1, ys, ls] = high

    for k in range(3):
        own_terms(k)
    heard(0)
    hello(1)

    def y_copy(k, d, h):
        j = lax.rem(i + d, n_inst)
        at = pl.multiple_of(start_of(j) * cols, cols)
        return remote(
            part.at[k, :, pl.ds(at, wy), lanes(h)], got.at[d - 1, k, :, :, lanes(h)],
            y_send.at[d - 1, k, h], y_recv.at[d - 1, k, h], (j, c),
        )

    for h in range(halves):
        for dc in (1, -1):
            @pl.when(inside(-dc))
            def _():
                halo_copy(dc, h).wait_recv()
        for k in range(3):
            halo_terms(k, h)
            for d in range(1, n_inst):
                y_copy(k, d, h).start()
        if h == 0:
            shift_rows()
    heard(1)
    hello(2)

    x_moves = {1: (3, 1, 2), -1: (3, 5, 2), 2: (4, 0, 1), -2: (3, 7, 1)}

    def x_copy(k, dc, h):
        src, dst, rows = x_moves[dc]
        slot = sorted(x_moves).index(dc)
        return remote(
            u0.at[k, pl.ds(src, rows), :, lanes(h)], u0.at[k, pl.ds(dst, rows), :, lanes(h)],
            x_send.at[slot, k, h], x_recv.at[slot, k, h], (i, c + dc),
        )

    my_at = pl.multiple_of(start_of(i) * cols, cols)
    for h in range(halves):
        for k in range(3):
            for d in range(1, n_inst):
                y_copy(k, d, h).wait_recv()
            total = part[k, :, pl.ds(my_at, wy), lanes(h)]
            for d in range(1, n_inst):
                total = total + got[d - 1, k, :, :, lanes(h)]
            u0[k, 3:5, :, lanes(h)] = total
            for dc in x_moves:
                @pl.when(inside(dc))
                def _():
                    x_copy(k, dc, h).start()

    for number in range(2, len(reaches)):
        heard(number)
        hello(number + 1)

    for dj, dc in sh_moves:
        @pl.when(sh_valid(dj, dc))
        def _():
            sh_copy(dj, dc).wait_send()
    for dc in (1, -1):
        @pl.when(inside(-dc))
        def _():
            sh_rows_copy(dc).wait_recv()

    for h in range(halves):
        for k in range(3):
            for dc in x_moves:
                @pl.when(inside(-dc))
                def _():
                    x_copy(k, dc, h).wait_recv()

    shape = (wy, nz)
    y_at = lax.broadcasted_iota(jnp.int32, shape, 0)
    z_at = lax.broadcasted_iota(jnp.int32, shape, 1)
    edges = (y_at == 0, y_at == wy - 1, z_at == 0, z_at == nz - 1)

    def valid_row(row):
        place = 2 * c + row - HALO
        return (place >= 0) & (place < 2 * n_cell)

    apply_operator(u0, u1, sh, 1, 6, valid_row, edges)
    apply_operator(u1, u2, sh, 2, 5, valid_row, edges)
    apply_operator(u2, u3, sh, 3, 4, valid_row, edges)

    basis = (u0, u1, u2, u3)
    lane = lax.broadcasted_iota(jnp.int32, (1, 128), 1)
    packed = jnp.zeros((1, 128), F32)
    for m in range(6):
        a, b = basis[m // 2], basis[(m + 1) // 2]
        total = None
        for k in range(3):
            for row in (3, 4):
                term = a[k, row] * b[k, row]
                total = term if total is None else total + term
        if window < n_inst:
            total = jnp.where((y_at >= own_at) & (y_at < own_at + cols), total, 0.0)
        value = jnp.sum(jnp.sum(total, axis=0, keepdims=True), axis=1, keepdims=True)
        packed = jnp.where(lane == m, value, packed)

    def gather_sum(packed, slot, buffer, send, recv, count, device):
        row_out[slot] = packed
        moves = [
            remote(row_out.at[slot], buffer.at[d - 1], send.at[d - 1], recv.at[d - 1], device(d))
            for d in range(1, count)
        ]
        for move in moves:
            move.start()
        total = packed
        for d, move in enumerate(moves):
            move.wait_recv()
            total = total + buffer[d]
        for move in moves:
            move.wait_send()
        return total

    packed = gather_sum(
        packed, 0, gath, g_send, g_recv, n_cell, lambda d: (i, lax.rem(c + d, n_cell))
    )
    if window < n_inst:
        packed = gather_sum(
            packed, 1, gath2, h_send, h_recv, n_inst, lambda d: (lax.rem(i + d, n_inst), c)
        )
    mu = [
        jnp.sum(jnp.where(lane == m, packed, 0.0), axis=1, keepdims=True) for m in range(6)
    ]
    at_x, at_r = coefficients(mu)

    own = pl.ds(own_at, cols)
    for k in range(3):
        for row in range(2):
            b = [basis[j][k, row + 3, own] for j in range(4)]
            x_ref[k, row] = at_x[0] * b[0] + at_x[1] * b[1] + at_x[2] * b[2]
            r_ref[k, row] = at_r[0] * b[0] + at_r[1] * b[1] + at_r[2] * b[2] + at_r[3] * b[3]

    for dc in (1, -1):
        @pl.when(inside(dc))
        def _():
            sh_rows_copy(dc).wait_send()
    for h in range(halves):
        for dc in (1, -1):
            @pl.when(inside(dc))
            def _():
                halo_copy(dc, h).wait_send()
        for k in range(3):
            for d in range(1, n_inst):
                y_copy(k, d, h).wait_send()
            for dc in x_moves:
                @pl.when(inside(dc))
                def _():
                    x_copy(k, dc, h).wait_send()


def hand_over(x_in, r_in, x_out, r_out, sem):
    moves = [
        pltpu.make_async_copy(x_in, x_out, sem.at[0]),
        pltpu.make_async_copy(r_in, r_out, sem.at[1]),
    ]
    for move in moves:
        move.start()
    for move in moves:
        move.wait()


def local(n_inst, n_cell, adjoint, flux_jac, shift):
    rows, cols, nz = shift.shape
    ny = adjoint.shape[3]
    window = min(3, n_inst)
    wy = window * cols
    field = pltpu.VMEM((3, rows + 2 * HALO, wy, nz), F32)
    dma = pltpu.SemaphoreType.DMA
    out = jax.ShapeDtypeStruct((3, rows, cols, nz), F32)
    peers = max(n_inst - 1, 1)
    answers = pl.pallas_call(
        functools.partial(kernel, n_inst, n_cell, cols, window),
        out_shape=(out, out),
        in_specs=[pl.BlockSpec(memory_space=pltpu.HBM)] * 3,
        out_specs=(pl.BlockSpec(memory_space=pltpu.VMEM),) * 2,
        scratch_shapes=[
            pltpu.VMEM(adjoint.shape, adjoint.dtype),
            pltpu.VMEM(flux_jac.shape, flux_jac.dtype),
            pltpu.VMEM((2,) + adjoint.shape[:2] + (ny, nz), adjoint.dtype),
            pltpu.VMEM((3, rows, ny, nz), F32),
            pltpu.VMEM((peers, 3, rows, wy, nz), F32),
            field, field, field, field,
            pltpu.VMEM((rows + 4, wy, nz), F32),
            pltpu.VMEM((2, 1, 128), F32),
            pltpu.VMEM((n_cell - 1, 1, 128), F32),
            pltpu.VMEM((peers, 1, 128), F32),
            dma((3,)),
            dma((2, 2)), dma((2, 2)),
            dma((2 * window - 1, 3)), dma((window, 3)),
            dma((peers, 3, 2)), dma((peers, 3, 2)),
            dma((4, 3, 2)), dma((4, 3, 2)),
            dma((n_cell - 1,)), dma((n_cell - 1,)),
            dma((peers,)), dma((peers,)),
            pltpu.SemaphoreType.REGULAR((6,)),
            dma((2,)), dma((2,)),
        ],
        compiler_params=pltpu.CompilerParams(
            collective_id=0, has_side_effects=True, vmem_limit_bytes=VMEM_GRANT
        ),
    )(*[pltpu.with_memory_space_constraint(a, pltpu.HBM) for a in (adjoint, flux_jac, shift)])
    return pl.pallas_call(
        hand_over,
        out_shape=(out, out),
        in_specs=[pl.BlockSpec(memory_space=pltpu.VMEM)] * 2,
        out_specs=(pl.BlockSpec(memory_space=pltpu.HBM),) * 2,
        scratch_shapes=[dma((2,))],
        compiler_params=pltpu.CompilerParams(vmem_limit_bytes=1 << 20),
    )(*answers)


def solution(mesh):
    placed = (
        P("inst", None, "cell", None, None),
        P("inst", None, None, "cell", None, None),
        P("cell", "inst", None),
    )
    return jax.shard_map(
        functools.partial(local, mesh.shape["inst"], mesh.shape["cell"]),
        mesh=mesh,
        in_specs=placed,
        out_specs=(P(None, "cell", "inst", None), P(None, "cell", "inst", None)),
        check_vma=False,
    )
```

```python
import functools

import jax
import jax.numpy as jnp
from jax import lax
from jax.experimental import pallas as pl
from jax.experimental.pallas import tpu as pltpu
from jax.sharding import PartitionSpec as P

ITERS = 3
LAME = 1.5
CENTER = 10.0
SPREAD = 8.0
HALO = 3
VMEM_GRANT = 24 << 20
MESH = pl.DeviceIdType.MESH
F32 = jnp.float32


def remote(src, dst, send_sem, recv_sem, device):
    return pltpu.make_async_remote_copy(
        src_ref=src,
        dst_ref=dst,
        send_sem=send_sem,
        recv_sem=recv_sem,
        device_id=device,
        device_id_type=MESH,
    )


def apply_operator(src, dst, sh, lo, hi, valid_row, edges):
    y_first, y_last, z_first, z_last = edges
    wy, nz = src.shape[2], src.shape[3]

    def up_y(v):
        return jnp.where(y_last, 0.0, pltpu.roll(v, wy - 1, 0))

    def down_y(v):
        return jnp.where(y_first, 0.0, pltpu.roll(v, 1, 0))

    def up_z(v):
        return jnp.where(z_last, 0.0, pltpu.roll(v, nz - 1, 1))

    def down_z(v):
        return jnp.where(z_first, 0.0, pltpu.roll(v, 1, 1))

    before = None
    for row in range(lo - 1, hi + 1):
        fields = [src[k, row] for k in range(3)]
        uy, uz = up_y(fields[1]), up_z(fields[2])
        dv = (src[0, row + 1] - fields[0]) + (uy - fields[1]) + (uz - fields[2])
        dv = jnp.where(valid_row(row), dv, 0.0)
        if row >= lo:
            diag = sh[row - 1] + (6.0 - CENTER)
            shifted = [before, down_y(dv), down_z(dv)]
            for k in range(3):
                u = fields[k]
                beside = src[k, row - 1] + src[k, row + 1]
                beside = beside + (uy if k == 1 else up_y(u)) + down_y(u)
                beside = beside + (uz if k == 2 else up_z(u)) + down_z(u)
                out = (diag * u - beside + LAME * (shifted[k] - dv)) * (1.0 / SPREAD)
                dst[k, row] = jnp.where(valid_row(row), out, 0.0)
        before = dv


def energy(src, sh, edges):
    _, y_last, _, z_last = edges
    wy, nz = src.shape[2], src.shape[3]
    total = None
    for row in (3, 4):
        dv = None
        for k in range(3):
            v = src[k, row]
            above = (
                src[k, row + 1],
                jnp.where(y_last, 0.0, pltpu.roll(v, wy - 1, 0)),
                jnp.where(z_last, 0.0, pltpu.roll(v, nz - 1, 1)),
            )
            step = above[k] - v
            dv = step if dv is None else dv + step
            diag = sh[row - 1] + (6.0 - CENTER)
            term = v * (diag * v - 2.0 * (above[0] + above[1] + above[2]))
            total = term if total is None else total + term
        total = total + LAME * (dv * dv)
    return total * (1.0 / SPREAD)


def coefficients(mu):
    def inner(a, b, skip=0):
        total = None
        for p, x in enumerate(a):
            for q, y in enumerate(b):
                if x is None or y is None:
                    continue
                term = x * y * mu[p + q]
                total = term if total is None else total + term
        return total

    def times(a):
        return [
            (CENTER * a[j] if j < len(a) else 0.0) + (SPREAD * a[j - 1] if j > 0 else 0.0)
            for j in range(len(a) + 1)
        ]

    one = jnp.ones_like(mu[0])
    solution_at, residual, direction = [], [one], [one]
    norm_now = mu[0]
    for sweep in range(ITERS):
        image = times(direction)
        alpha = norm_now / inner(direction, image)
        solution_at = [
            (solution_at[j] if j < len(solution_at) else 0.0) + alpha * direction[j]
            for j in range(len(direction))
        ]
        residual = [
            (residual[j] if j < len(residual) else 0.0) - alpha * image[j]
            for j in range(len(image))
        ]
        if sweep + 1 < ITERS:
            norm_next = inner(residual, residual)
            ratio = norm_next / norm_now
            direction = [
                residual[j] + (ratio * direction[j] if j < len(direction) else 0.0)
                for j in range(len(residual))
            ]
            norm_now = norm_next
    return solution_at, residual


def kernel(
    n_inst, n_cell, cols, window,
    adj_hbm, flux_hbm, shift_hbm, x_ref, r_ref,
    adj, flux, halo, part, got, u0, u1, u2, u3, sh, row_out, gath, gath2,
    load_sem, halo_send, halo_recv, sh_send, sh_recv, y_send, y_recv,
    x_send, x_recv, g_send, g_recv, h_send, h_recv, near, shx_send, shx_recv,
):
    i, c = lax.axis_index("inst"), lax.axis_index("cell")
    wy = window * cols
    nv = adj.shape[0] * adj.shape[1]
    nz = adj.shape[-1]

    halves = 2 if nz % 256 == 0 else 1

    def lanes(h):
        return slice(h * (nz // halves), (h + 1) * (nz // halves))

    def start_of(j):
        return jnp.clip(j - 1, 0, n_inst - window)

    own_at = pl.multiple_of((i - start_of(i)) * cols, cols)

    loads = [
        pltpu.make_async_copy(adj_hbm, adj, load_sem.at[0]),
        pltpu.make_async_copy(flux_hbm, flux, load_sem.at[1]),
        pltpu.make_async_copy(shift_hbm, sh.at[pl.ds(2, 2), pl.ds(own_at, cols)], load_sem.at[2]),
    ]
    for load in loads:
        load.start()

    def inside(dc):
        return (c + dc >= 0) & (c + dc < n_cell)

    barrier = pltpu.get_barrier_semaphore()
    expected = n_inst - 1
    for dc in (-1, 1, -2, 2):
        expected = expected + jnp.where(inside(dc), 1, 0)

        @pl.when(inside(dc))
        def _():
            pl.semaphore_signal(barrier, inc=1, device_id=(i, c + dc), device_id_type=MESH)

    for d in range(1, n_inst):
        pl.semaphore_signal(barrier, inc=1, device_id=(lax.rem(i + d, n_inst), c), device_id_type=MESH)
    pl.semaphore_wait(barrier, expected)

    reaches = [r for r in (2, 4, 8, 16, 32, 64) if r < n_cell]

    def hello(number):
        if number < len(reaches):
            for dc in (-reaches[number], reaches[number]):
                @pl.when(inside(dc))
                def _():
                    pl.semaphore_signal(
                        near.at[number], inc=1, device_id=(i, c + dc), device_id_type=MESH
                    )

    def heard(number):
        if number < len(reaches):
            count = 0
            for dc in (-reaches[number], reaches[number]):
                count = count + jnp.where(inside(dc), 1, 0)
            pl.semaphore_wait(near.at[number], count)

    def halo_copy(dc, h):
        side = 0 if dc == 1 else 1
        return remote(
            adj.at[:, :, 1 if dc == 1 else 0, :, lanes(h)], halo.at[side, :, :, :, lanes(h)],
            halo_send.at[side, h], halo_recv.at[side, h], (i, c + dc),
        )

    loads[0].wait()

    for h in range(halves):
        for dc in (1, -1):
            @pl.when(inside(dc))
            def _():
                halo_copy(dc, h).start()
    hello(0)

    def sh_copy(dj, dc):
        j = i + dj
        slot = jnp.clip(i - start_of(j), 0, window - 1)
        at = pl.multiple_of(slot * cols, cols)
        return remote(
            shift_hbm, sh.at[pl.ds(2 - 2 * dc, 2), pl.ds(at, cols)],
            sh_send.at[dj + window - 1, dc + 1], sh_recv.at[slot, dc + 1], (j, c + dc),
        )

    def sh_valid(dj, dc):
        j = i + dj
        first = start_of(j)
        return (j >= 0) & (j < n_inst) & inside(dc) & (i >= first) & (i < first + window)

    sh_moves = [(dj, 0) for dj in range(-(window - 1), window) if dj != 0]
    for dj, dc in sh_moves:
        @pl.when(sh_valid(dj, dc))
        def _():
            sh_copy(dj, dc).start()

    def sh_rows_copy(dc):
        side = 0 if dc == 1 else 1
        return remote(
            sh.at[2:4], sh.at[pl.ds(2 - 2 * dc, 2)],
            shx_send.at[side], shx_recv.at[side], (i, c + dc),
        )

    def shift_rows():
        loads[2].wait()
        for slot in range(window):
            @pl.when(start_of(i) + slot != i)
            def _():
                remote(
                    shift_hbm, sh.at[2:4, pl.ds(slot * cols, cols)],
                    sh_send.at[0, 0], sh_recv.at[slot, 1], (i, c),
                ).wait_recv()
        for dc in (1, -1):
            @pl.when(inside(dc))
            def _():
                sh_rows_copy(dc).start()

    @pl.when(c == 0)
    def _():
        halo[0] = jnp.zeros_like(halo[0])
        sh[0:2] = jnp.zeros_like(sh[0:2])
        u0[:, 0:3] = jnp.zeros_like(u0[:, 0:3])

    @pl.when(c == 1)
    def _():
        u0[:, 0:1] = jnp.zeros_like(u0[:, 0:1])

    @pl.when(c == n_cell - 1)
    def _():
        halo[1] = jnp.zeros_like(halo[1])
        sh[4:6] = jnp.zeros_like(sh[4:6])
        u0[:, 5:8] = jnp.zeros_like(u0[:, 5:8])

    @pl.when(c == n_cell - 2)
    def _():
        u0[:, 7:8] = jnp.zeros_like(u0[:, 7:8])

    loads[1].wait()

    n_v = adj.shape[1]

    def own_terms(k):
        for y0 in range(0, adj.shape[3], 16):
            ys = slice(y0, y0 + 16)
            low, high = None, None
            for v in range(nv):
                a, b = v // n_v, v % n_v
                t0 = flux[a, b, k, 0, ys].astype(F32) * adj[a, b, 1, ys].astype(F32)
                t1 = flux[a, b, k, 1, ys].astype(F32) * adj[a, b, 0, ys].astype(F32)
                low = t0 if low is None else low + t0
                high = t1 if high is None else high + t1
            part[k, 0, ys] = low
            part[k, 1, ys] = -high

    def halo_terms(k, h):
        ls = lanes(h)
        for y0 in range(0, adj.shape[3], 16):
            ys = slice(y0, y0 + 16)
            low, high = part[k, 0, ys, ls], part[k, 1, ys, ls]
            for v in range(nv):
                a, b = v // n_v, v % n_v
                f0, f1 = flux[a, b, k, 0, ys, ls], flux[a, b, k, 1, ys, ls]
                low = low - f0.astype(F32) * halo[0, a, b, ys, ls].astype(F32)
                high = high + f1.astype(F32) * halo[1, a, b, ys, ls].astype(F32)
            part[k, 0, ys, ls] = low
            part[k, 1, ys, ls] = high

    for k in range(3):
        own_terms(k)
    heard(0)
    hello(1)

    def y_copy(k, d, h):
        j = lax.rem(i + d, n_inst)
        at = pl.multiple_of(start_of(j) * cols, cols)
        return remote(
            part.at[k, :, pl.ds(at, wy), lanes(h)], got.at[d - 1, k, :, :, lanes(h)],
            y_send.at[d - 1, k, h], y_recv.at[d - 1, k, h], (j, c),
        )

    for h in range(halves):
        for dc in (1, -1):
            @pl.when(inside(-dc))
            def _():
                halo_copy(dc, h).wait_recv()
        for k in range(3):
            halo_terms(k, h)
            for d in range(1, n_inst):
                y_copy(k, d, h).start()
        if h == 0:
            shift_rows()
    heard(1)
    hello(2)

    x_moves = {1: (3, 1, 2), -1: (3, 5, 2), 2: (4, 0, 1), -2: (3, 7, 1)}

    def x_copy(k, dc, h):
        src, dst, rows = x_moves[dc]
        slot = sorted(x_moves).index(dc)
        return remote(
            u0.at[k, pl.ds(src, rows), :, lanes(h)], u0.at[k, pl.ds(dst, rows), :, lanes(h)],
            x_send.at[slot, k, h], x_recv.at[slot, k, h], (i, c + dc),
        )

    my_at = pl.multiple_of(start_of(i) * cols, cols)
    for h in range(halves):
        for k in range(3):
            for d in range(1, n_inst):
                y_copy(k, d, h).wait_recv()
            total = part[k, :, pl.ds(my_at, wy), lanes(h)]
            for d in range(1, n_inst):
                total = total + got[d - 1, k, :, :, lanes(h)]
            u0[k, 3:5, :, lanes(h)] = total
            for dc in (1, -1, -2):
                @pl.when(inside(dc))
                def _():
                    x_copy(k, dc, h).start()

    for number in range(2, len(reaches)):
        heard(number)
        hello(number + 1)

    for dj, dc in sh_moves:
        @pl.when(sh_valid(dj, dc))
        def _():
            sh_copy(dj, dc).wait_send()
    for dc in (1, -1):
        @pl.when(inside(-dc))
        def _():
            sh_rows_copy(dc).wait_recv()

    def field_arrived(directions):
        for h in range(halves):
            for k in range(3):
                for dc in directions:
                    @pl.when(inside(-dc))
                    def _():
                        x_copy(k, dc, h).wait_recv()

    field_arrived((1, -1, -2))

    shape = (wy, nz)
    y_at = lax.broadcasted_iota(jnp.int32, shape, 0)
    z_at = lax.broadcasted_iota(jnp.int32, shape, 1)
    edges = (y_at == 0, y_at == wy - 1, z_at == 0, z_at == nz - 1)

    def valid_row(row):
        place = 2 * c + row - HALO
        return (place >= 0) & (place < 2 * n_cell)

    apply_operator(u0, u1, sh, 2, 6, valid_row, edges)
    apply_operator(u1, u2, sh, 3, 5, valid_row, edges)

    def rest():
        for h in range(halves):
            for k in range(3):
                @pl.when(inside(2))
                def _():
                    x_copy(k, 2, h).start()

        field_arrived((2,))
        apply_operator(u0, u1, sh, 1, 1, valid_row, edges)
        apply_operator(u1, u2, sh, 2, 2, valid_row, edges)
        apply_operator(u2, u3, sh, 3, 4, valid_row, edges)

    basis = (u0, u1, u2, u3)
    lane = lax.broadcasted_iota(jnp.int32, (1, 128), 1)
    packed = jnp.zeros((1, 128), F32)
    for m in range(6):
        total = energy(u2, sh, edges) if m == 5 else None
        a, b = basis[m // 2], basis[(m + 1) // 2]
        for k in range(3 if m < 5 else 0):
            for row in (3, 4):
                term = a[k, row] * b[k, row]
                total = term if total is None else total + term
        if window < n_inst:
            total = jnp.where((y_at >= own_at) & (y_at < own_at + cols), total, 0.0)
        value = jnp.sum(jnp.sum(total, axis=0, keepdims=True), axis=1, keepdims=True)
        packed = jnp.where(lane == m, value, packed)

    def gather_sum(packed, slot, buffer, send, recv, count, device, meanwhile):
        row_out[slot] = packed
        moves = [
            remote(row_out.at[slot], buffer.at[d - 1], send.at[d - 1], recv.at[d - 1], device(d))
            for d in range(1, count)
        ]
        for move in moves:
            move.start()
        meanwhile()
        total = packed
        for d, move in enumerate(moves):
            move.wait_recv()
            total = total + buffer[d]
        for move in moves:
            move.wait_send()
        return total

    packed = gather_sum(
        packed, 0, gath, g_send, g_recv, n_cell, lambda d: (i, lax.rem(c + d, n_cell)), rest
    )
    if window < n_inst:
        packed = gather_sum(
            packed, 1, gath2, h_send, h_recv, n_inst, lambda d: (lax.rem(i + d, n_inst), c),
            lambda: None,
        )
    mu = [
        jnp.sum(jnp.where(lane == m, packed, 0.0), axis=1, keepdims=True) for m in range(6)
    ]
    at_x, at_r = coefficients(mu)

    own = pl.ds(own_at, cols)
    for k in range(3):
        for row in range(2):
            b = [basis[j][k, row + 3, own] for j in range(4)]
            x_ref[k, row] = at_x[0] * b[0] + at_x[1] * b[1] + at_x[2] * b[2]
            r_ref[k, row] = at_r[0] * b[0] + at_r[1] * b[1] + at_r[2] * b[2] + at_r[3] * b[3]

    for dc in (1, -1):
        @pl.when(inside(dc))
        def _():
            sh_rows_copy(dc).wait_send()
    for h in range(halves):
        for dc in (1, -1):
            @pl.when(inside(dc))
            def _():
                halo_copy(dc, h).wait_send()
        for k in range(3):
            for d in range(1, n_inst):
                y_copy(k, d, h).wait_send()
            for dc in x_moves:
                @pl.when(inside(dc))
                def _():
                    x_copy(k, dc, h).wait_send()


def hand_over(x_in, r_in, x_out, r_out, sem):
    moves = [
        pltpu.make_async_copy(x_in, x_out, sem.at[0]),
        pltpu.make_async_copy(r_in, r_out, sem.at[1]),
    ]
    for move in moves:
        move.start()
    for move in moves:
        move.wait()


def local(n_inst, n_cell, adjoint, flux_jac, shift):
    rows, cols, nz = shift.shape
    ny = adjoint.shape[3]
    window = min(3, n_inst)
    wy = window * cols
    field = pltpu.VMEM((3, rows + 2 * HALO, wy, nz), F32)
    dma = pltpu.SemaphoreType.DMA
    out = jax.ShapeDtypeStruct((3, rows, cols, nz), F32)
    peers = max(n_inst - 1, 1)
    answers = pl.pallas_call(
        functools.partial(kernel, n_inst, n_cell, cols, window),
        out_shape=(out, out),
        in_specs=[pl.BlockSpec(memory_space=pltpu.HBM)] * 3,
        out_specs=(pl.BlockSpec(memory_space=pltpu.VMEM),) * 2,
        scratch_shapes=[
            pltpu.VMEM(adjoint.shape, adjoint.dtype),
            pltpu.VMEM(flux_jac.shape, flux_jac.dtype),
            pltpu.VMEM((2,) + adjoint.shape[:2] + (ny, nz), adjoint.dtype),
            pltpu.VMEM((3, rows, ny, nz), F32),
            pltpu.VMEM((peers, 3, rows, wy, nz), F32),
            field, field, field, field,
            pltpu.VMEM((rows + 4, wy, nz), F32),
            pltpu.VMEM((2, 1, 128), F32),
            pltpu.VMEM((n_cell - 1, 1, 128), F32),
            pltpu.VMEM((peers, 1, 128), F32),
            dma((3,)),
            dma((2, 2)), dma((2, 2)),
            dma((2 * window - 1, 3)), dma((window, 3)),
            dma((peers, 3, 2)), dma((peers, 3, 2)),
            dma((4, 3, 2)), dma((4, 3, 2)),
            dma((n_cell - 1,)), dma((n_cell - 1,)),
            dma((peers,)), dma((peers,)),
            pltpu.SemaphoreType.REGULAR((6,)),
            dma((2,)), dma((2,)),
        ],
        compiler_params=pltpu.CompilerParams(
            collective_id=0, has_side_effects=True, vmem_limit_bytes=VMEM_GRANT
        ),
    )(*[pltpu.with_memory_space_constraint(a, pltpu.HBM) for a in (adjoint, flux_jac, shift)])
    return pl.pallas_call(
        hand_over,
        out_shape=(out, out),
        in_specs=[pl.BlockSpec(memory_space=pltpu.VMEM)] * 2,
        out_specs=(pl.BlockSpec(memory_space=pltpu.HBM),) * 2,
        scratch_shapes=[dma((2,))],
        compiler_params=pltpu.CompilerParams(vmem_limit_bytes=1 << 20),
    )(*answers)


def solution(mesh):
    placed = (
        P("inst", None, "cell", None, None),
        P("inst", None, None, "cell", None, None),
        P("cell", "inst", None),
    )
    return jax.shard_map(
        functools.partial(local, mesh.shape["inst"], mesh.shape["cell"]),
        mesh=mesh,
        in_specs=placed,
        out_specs=(P(None, "cell", "inst", None), P(None, "cell", "inst", None)),
        check_vma=False,
    )
```
